32 devices in a mesh: wide: 8 (over z, y), narrow: 4 (over x, core).
Axes of the slice: x: 2, y: 2, z: 4, core: 2. Of those that a mesh axis runs over, the one named last changes fastest.
Arguments:
- tokens: bfloat16 [80, 1024, 768], P('wide', 'narrow'), may hold values from -12 to 12, as said below
- usable: int32 [80, 1024], P('wide', 'narrow'), may hold values from 0 to 1, as said below
- conv_weight: bfloat16 [2304, 384], P(('wide', 'narrow')), may hold values from -0.125 to 0.125
- point_weight: bfloat16 [768, 384], P(('wide', 'narrow')), may hold values from -0.3125 to 0.3125
- head_weight: bfloat16 [768, 5313], P(('wide', 'narrow')), may hold values from -0.21875 to 0.21875
- first_gain: float32 [768], replicated, may hold values from 0.1 to 1.9
- first_shift: float32 [768], replicated, may hold values from -3 to 3
- second_gain: float32 [384], replicated, may hold values from 0.1 to 1.9
- second_shift: float32 [384], replicated, may hold values from -3 to 3
- point_bias: float32 [768], replicated, may hold values from -2 to 2
- head_bias: float32 [5313], replicated, may hold values from -1 to 1
- cot_block: bfloat16 [80, 1024, 768], P('wide', 'narrow'), may hold values from -6 to 6
- cot_tracks: bfloat16 [80, 5313, 1024], P('wide', None, 'narrow'), may hold values from -6 to 6
Outputs:
- block_out: bfloat16 [80, 1024, 768], P('wide', 'narrow')
- tracks_out: bfloat16 [80, 5313, 1024], P('wide', None, 'narrow')
- grad_tokens: float32 [80, 1024, 768], P('wide', 'narrow')
- grad_conv: float32 [2304, 384], P(('wide', 'narrow'))
- grad_point: float32 [768, 384], P(('wide', 'narrow'))
- grad_head: float32 [768, 5313], P(('wide', 'narrow'))
- grad_first_gain: float32 [768], replicated
- grad_first_shift: float32 [768], replicated
- grad_second_gain: float32 [384], replicated
- grad_second_shift: float32 [384], replicated
- grad_point_bias: float32 [768], replicated
- grad_head_bias: float32 [5313], replicated
The draws below stay inside these ranges and needn't reach their ends.
Inputs may be any that keep to these rules, and one draw needn't show every extreme that they name: 1 marks a usable bin. Blacklisted runs of 16 aligned bins and scattered unmappable bins are 0, with a blacklist rate that differs from window to window; the first bin of every window is usable. `tokens`: activations of order one whose scale grows along the bins and windows.
All inputs are finite; a program needn't handle non-finite values.
Results may differ from the reference program's by a relative error of at most 0.008.
Values may be sent and summed in bfloat16 or wider, within the bound.
No kernel may reach another device: no remote copies, remote signals or barrier semaphores. Data moves between devices by JAX's collectives and lax.ppermute only.
A program may use at most 256 MiB of HBM per device.

```python
import jax
import jax.numpy as jnp
from jax import lax

C = 768
H = 384
TRACKS = 5313
WINDOW_LENGTH = 1024
DILATION_STEP = 11
WINDOWS = 80


def draw_usable(key, part):
    key_rate = jax.random.fold_in(key, 11)
    key_runs = jax.random.fold_in(key, 12)
    key_lone = jax.random.fold_in(key, 13)
    rates = jax.random.randint(key_rate, (WINDOWS, 1), 0, 60)
    runs = jax.random.randint(key_runs, (WINDOWS, WINDOW_LENGTH // 16), 0, 100)
    black = jnp.repeat(runs < rates, 16, axis=1)
    lone = jax.random.randint(key_lone, (WINDOWS, WINDOW_LENGTH), 0, 12) == 0
    keep = jnp.logical_not(jnp.logical_or(black, lone))
    first = jnp.arange(WINDOW_LENGTH)[None, :] == 0
    return jnp.logical_or(keep, first).astype(jnp.int32)


def draw_tokens(key, part):
    key_offset = jax.random.fold_in(key, 21)
    key_noise = jax.random.fold_in(key, 22)
    window_pos = jnp.arange(WINDOWS, dtype=jnp.float32)[:, None] * WINDOW_LENGTH
    bin_pos = jnp.arange(WINDOW_LENGTH, dtype=jnp.float32)[None, :]
    ramp = 0.6 + 1.2 * (window_pos + bin_pos) / (WINDOWS * WINDOW_LENGTH)
    offset = jnp.clip(jax.random.normal(key_offset, (C,), jnp.float32), -3.0, 3.0) * 0.8
    noise = jnp.clip(jax.random.normal(key_noise, (WINDOWS, WINDOW_LENGTH, C), jnp.float32), -4.0, 4.0)
    values = (offset + noise) * ramp[:, :, None]
    return values.astype(jnp.bfloat16)


def level_of(own_key, extent, shards, least, high):
    def one(position, shards_of):
        steps = jax.random.uniform(jax.random.fold_in(jax.random.fold_in(own_key, 6), position), (shards_of,), jnp.float32, least / len(shards), high / len(shards))
        return jnp.repeat(jnp.exp(steps), extent[position] // shards_of).reshape((-1,) + (1,) * (len(extent) - position - 1))

    level = one(*shards[0])
    for cut in shards[1:]:
        level = level * one(*cut)
    return level


def normal_values(rng, dims, deviation, bound, split=(), kind=jnp.bfloat16):
    drawn = jax.random.normal(rng, dims, jnp.float32) * deviation
    if len(split) > 0:
        drawn = level_of(rng, dims, split, -0.22, 0.18) * drawn
    return jnp.clip(drawn, min=-bound, max=bound).astype(kind)


def setup_inputs(seed: int = 0) -> dict:
    splits = jax.random.split(jax.random.key(seed), 14)
    return {
        "tokens": draw_tokens(jax.random.fold_in(splits[13], 71), 0),
        "usable": draw_usable(jax.random.fold_in(splits[13], 71), 0),
        "conv_weight": normal_values(splits[2], (3 * C, H), (3 * C) ** -0.5, 0.125, ((0, 32),)),
        "point_weight": normal_values(splits[3], (C, H), H ** -0.5, 0.3125, ((0, 32),)),
        "head_weight": normal_values(splits[4], (C, TRACKS), C ** -0.5, 0.21875, ((0, 32),)),
        "first_gain": jnp.clip(1.0 + 0.18 * jax.random.normal(splits[5], (C,), jnp.float32), 0.1, 1.9),
        "first_shift": normal_values(splits[6], (C,), 0.5, 3.0, (), jnp.float32),
        "second_gain": jnp.clip(1.0 + 0.18 * jax.random.normal(splits[7], (H,), jnp.float32), 0.1, 1.9),
        "second_shift": normal_values(splits[8], (H,), 0.5, 3.0, (), jnp.float32),
        "point_bias": normal_values(splits[9], (C,), 0.3, 2.0, (), jnp.float32),
        "head_bias": jnp.clip(jax.random.uniform(splits[10], (TRACKS,), jnp.float32, -1.0, 1.0), -1.0, 1.0),
        "cot_block": normal_values(splits[11], (WINDOWS, WINDOW_LENGTH, C), 1.0, 6.0, ((0, 8), (1, 4))),
        "cot_tracks": normal_values(splits[12], (WINDOWS, TRACKS, WINDOW_LENGTH), 1.0, 6.0, ((0, 8), (2, 4))),
    }


@jax.custom_vjp
def low(v):
    return lax.optimization_barrier(v.astype(jnp.bfloat16)).astype(jnp.float32)

@jax.custom_vjp
def low_back(v):
    return v

def low_keep(v):
    return (low(v), None)

def low_pass(kept, grad):
    return (grad,)

def back_keep(v):
    return (v, None)

def back_low(kept, grad):
    return (low(grad),)
low.defvjp(low_keep, low_pass)
low_back.defvjp(back_keep, back_low)
epsilon = 1e-05

def masked_norm(values, weight):
    counted = jnp.sum(weight)
    mean_value = lax.optimization_barrier(jnp.sum(values * weight, axis=(0, 1))) / counted
    centred = values - mean_value
    spread = lax.optimization_barrier(jnp.sum(weight * centred * centred, axis=(0, 1))) / counted
    return centred * lax.rsqrt(spread + epsilon)

def reference(tokens, usable, conv_weight, point_weight, head_weight, first_gain, first_shift, second_gain, second_shift, point_bias, head_bias, cot_block, cot_tracks):
    weight = usable.astype(jnp.float32)[:, :, None]
    highest_precision = lax.Precision.HIGHEST

    def forward(source, conv_full, point_full, head_full, gain_one, shift_one, gain_two, shift_two, bias_point, bias_head):
        first_inner = masked_norm(source, weight) * gain_one + shift_one
        first_activated = low(jax.nn.gelu(first_inner))
        padded_input = jnp.pad(first_activated, ((0, 0), (DILATION_STEP, DILATION_STEP), (0, 0)))
        convolution_kernel = conv_full.reshape(3, C, H)
        hidden_state = jnp.einsum('ldo,ov->ldv', padded_input[:, 0:WINDOW_LENGTH], convolution_kernel[0], precision=highest_precision)
        for kernel_position in range(1, 3):
            hidden_state = hidden_state + jnp.einsum('ldo,ov->ldv', padded_input[:, kernel_position * DILATION_STEP:kernel_position * DILATION_STEP + WINDOW_LENGTH], convolution_kernel[kernel_position], precision=highest_precision)
        hidden_state = low_back(hidden_state)
        second_inner = masked_norm(hidden_state, weight) * gain_two + shift_two
        second_active = low(jax.nn.gelu(second_inner))
        branch = low_back(jnp.einsum('wbh,ch->wbc', second_active, point_full, precision=highest_precision) + bias_point)
        block = low(source + branch)

        def head_block(window_rows):
            logits = jnp.einsum('bc,ct->tb', window_rows, head_full, precision=highest_precision) + bias_head[:, None]
            return jax.nn.softplus(low_back(logits))
        tracks = lax.map(jax.checkpoint(head_block), block)
        return (block, tracks)
    inputs = (tokens.astype(jnp.float32), conv_weight.astype(jnp.float32), point_weight.astype(jnp.float32), head_weight.astype(jnp.float32), first_gain, first_shift, second_gain, second_shift, point_bias, head_bias)
    (block, tracks), pull = jax.vjp(forward, *inputs)
    grads = pull((cot_block.astype(jnp.float32) * weight, cot_tracks.astype(jnp.float32) * usable.astype(jnp.float32)[:, None, :]))
    return (block.astype(jnp.bfloat16), tracks.astype(jnp.bfloat16), grads[0], grads[1], grads[2], grads[3], grads[4], grads[5], grads[6], grads[7], grads[8], grads[9])
```

```python
import jax
import jax.numpy as jnp
from jax import lax
from jax.sharding import PartitionSpec as P

DILATION_STEP = 11
BOTH = ("wide", "narrow")
F32 = jnp.float32
BF16 = jnp.bfloat16


epsilon = 1e-05


def axis_bits():
    found = []
    for axis in ("narrow", "wide"):
        count = lax.axis_size(axis)
        assert count & (count - 1) == 0
        found += [(axis, count, bit) for bit in range(count.bit_length() - 1)]
    return found


def swap(value, axis, count, bit):
    return lax.ppermute(value, axis, [(i, i ^ (1 << bit)) for i in range(count)])


def my_bit(axis, bit):
    return (lax.axis_index(axis) >> bit) & 1


def sum_all(value):
    for axis, count, bit in axis_bits():
        value = value + swap(value, axis, count, bit)
    return value


def gather_rows(shard):
    rows, columns = shard.shape
    held = shard[None]
    for axis, count, bit in reversed(axis_bits()):
        other = swap(held, axis, count, bit)
        low = my_bit(axis, bit) == 0
        first = jnp.where(low, held, other)
        second = jnp.where(low, other, held)
        held = jnp.stack([first, second], axis=1).reshape(-1, rows, columns)
    return held


def scatter_rows(value):
    rows, columns = value.shape[1:]
    for axis, count, bit in axis_bits():
        pairs = value.reshape(-1, 2, rows, columns)
        mine = my_bit(axis, bit)
        send = lax.dynamic_index_in_dim(pairs, 1 - mine, axis=1, keepdims=False)
        keep = lax.dynamic_index_in_dim(pairs, mine, axis=1, keepdims=False)
        got = swap(send, axis, count, bit)
        value = (keep.astype(F32) + got.astype(F32)).astype(value.dtype)
    return value[0]


def halos(first, last, axis):
    count = lax.axis_size(axis)
    up = [(i, i + 1) for i in range(count - 1)]
    down = [(i + 1, i) for i in range(count - 1)]
    return lax.ppermute(last, axis, up), lax.ppermute(first, axis, down)


def edges(value):
    return value[:, :DILATION_STEP], value[:, value.shape[1] - DILATION_STEP :]


def norm_stats(values, weight):
    channels = values.shape[-1]
    number = jnp.sum(weight)
    total = jnp.sum(values * weight, axis=(0, 1))
    centred = values - total / jnp.maximum(number, 1.0)
    spread = jnp.sum(weight * centred * centred, axis=(0, 1))
    packed = jnp.stack([total, spread, jnp.broadcast_to(number, (channels,))])
    for axis, count, bit in axis_bits():
        other = swap(packed, axis, count, bit)
        n_a, n_b = packed[2], other[2]
        both = n_a + n_b
        gap = packed[0] / jnp.maximum(n_a, 1.0) - other[0] / jnp.maximum(n_b, 1.0)
        merged = packed[1] + other[1] + gap * gap * (n_a * n_b / jnp.maximum(both, 1.0))
        packed = jnp.stack([packed[0] + other[0], merged, both])
    counted = packed[2]
    return packed[0] / counted, lax.rsqrt(packed[1] / counted + epsilon), counted


def gelu_back(preact, upstream):
    return jax.vjp(jax.nn.gelu, preact)[1](upstream)[0]


def norm_back(grad_inner, normed, scale_inv, gain, grad_gain, grad_shift, weight, counted):
    grad_normed = grad_inner * gain
    return scale_inv * (
        grad_normed - weight / counted * (gain * grad_shift + normed * gain * grad_gain)
    )


def shards(
    tokens,
    usable,
    conv_weight,
    point_weight,
    head_weight,
    first_gain,
    first_shift,
    second_gain,
    second_shift,
    point_bias,
    head_bias,
    cot_block,
    cot_tracks,
):
    windows, bins, channels = tokens.shape
    filters = conv_weight.shape[1]
    devices = lax.axis_size("wide") * lax.axis_size("narrow")
    own = channels // devices
    weight = usable.astype(F32)[:, :, None]
    row_weight = usable.astype(F32)[:, None, :]
    source = tokens.astype(F32)
    head_full = lax.all_gather(head_weight, BOTH, axis=0, tiled=True)
    small = gather_rows(
        jnp.concatenate([conv_weight.reshape(own, 3 * filters), point_weight], axis=1)
    )
    kernel = small[:, :, : 3 * filters].reshape(3, channels, filters)
    point_full = small[:, :, 3 * filters :].reshape(channels, filters)

    before, after = halos(*edges(tokens), "narrow")
    padded = jnp.concatenate([before, tokens, after], axis=1).astype(F32)
    place = lax.axis_index("narrow") * bins + jnp.arange(-DILATION_STEP, bins + DILATION_STEP)
    inside = (place >= 0) & (place < bins * lax.axis_size("narrow"))
    inside = inside[None, :, None]

    first_mean, first_scale, counted = norm_stats(source, weight)
    padded_inner = (padded - first_mean) * first_scale * first_gain + first_shift
    padded_input = jnp.where(inside, jax.nn.gelu(padded_inner), 0.0).astype(BF16)
    taps = [padded_input[:, k * DILATION_STEP : k * DILATION_STEP + bins] for k in range(3)]
    hidden = sum(
        jnp.einsum("ldo,ov->ldv", taps[k], kernel[k], preferred_element_type=F32) for k in range(3)
    )
    second_mean, second_scale, counted_two = norm_stats(hidden, weight)
    second_normed = (hidden - second_mean) * second_scale
    second_inner = second_normed * second_gain + second_shift
    second_active = jax.nn.gelu(second_inner).astype(BF16)
    branch = (
        jnp.einsum("wbh,ch->wbc", second_active, point_full, preferred_element_type=F32)
        + point_bias
    )
    block = (source + branch).astype(BF16)

    logits = jnp.einsum("wbc,ct->wtb", block, head_full, preferred_element_type=F32)
    logits = logits + head_bias[None, :, None]
    tracks = jax.nn.softplus(logits).astype(BF16)
    grad_logits = (cot_tracks.astype(F32) * row_weight * jax.nn.sigmoid(logits)).astype(BF16)
    grad_head_local = jnp.einsum(
        "wbc,wtb->ct", block, grad_logits, preferred_element_type=F32
    ).astype(BF16)
    grad_head = scatter_rows(grad_head_local.reshape(devices, own, -1)).astype(F32)
    grad_block = jnp.einsum("wtb,ct->wbc", grad_logits, head_full, preferred_element_type=F32)
    grad_summed = cot_block.astype(F32) * weight + grad_block
    grad_branch = grad_summed.astype(BF16)
    grad_point_local = jnp.einsum(
        "wbc,wbh->ch", grad_branch, second_active, preferred_element_type=F32
    )
    grad_second_active = jnp.einsum(
        "wbc,ch->wbh", grad_branch, point_full, preferred_element_type=F32
    )
    grad_second_inner = gelu_back(second_inner, grad_second_active)
    before, after = halos(
        *edges(jnp.concatenate([grad_second_inner, second_normed], axis=2)), "narrow"
    )
    weight_before, weight_after = halos(*edges(weight[:, :, 0]), "narrow")
    sums = sum_all(
        jnp.concatenate(
            [
                jnp.sum(grad_second_inner * second_normed, axis=(0, 1)),
                jnp.sum(grad_second_inner, axis=(0, 1)),
                jnp.sum(grad_branch.astype(F32), axis=(0, 1)),
                jnp.sum(grad_logits.astype(F32), axis=(0, 2)),
            ]
        )
    )
    grad_second_gain = sums[:filters]
    grad_second_shift = sums[filters : 2 * filters]
    grad_point_bias = sums[2 * filters : 2 * filters + channels]
    grad_head_bias = sums[2 * filters + channels :]

    def hidden_back(inner, normed, row):
        return norm_back(
            inner,
            normed,
            second_scale,
            second_gain,
            grad_second_gain,
            grad_second_shift,
            row,
            counted[0],
        ).astype(BF16)

    hidden_gradient = hidden_back(grad_second_inner, second_normed, weight)
    padded_gradient = jnp.concatenate(
        [
            hidden_back(before[..., :filters], before[..., filters:], weight_before[:, :, None]),
            hidden_gradient,
            hidden_back(after[..., :filters], after[..., filters:], weight_after[:, :, None]),
        ],
        axis=1,
    )
    grad_taps = [
        jnp.einsum("wbc,wbh->ch", taps[k], hidden_gradient, preferred_element_type=F32)
        for k in range(3)
    ]
    grad_small = jnp.concatenate(
        [
            jnp.concatenate(grad_taps, axis=0).astype(BF16).reshape(devices, own, 3 * filters),
            grad_point_local.astype(BF16).reshape(devices, own, filters),
        ],
        axis=2,
    )
    grad_small = scatter_rows(grad_small).astype(F32)
    grad_conv = grad_small[:, : 3 * filters].reshape(3 * own, filters)
    grad_point = grad_small[:, 3 * filters :]

    grad_first_active = sum(
        jnp.einsum(
            "wbh,ch->wbc",
            padded_gradient[:, (2 - k) * DILATION_STEP : (2 - k) * DILATION_STEP + bins],
            kernel[k],
            preferred_element_type=F32,
        )
        for k in range(3)
    )
    first_normed = (source - first_mean) * first_scale
    first_inner = first_normed * first_gain + first_shift
    grad_first_inner = gelu_back(first_inner, grad_first_active)
    sums = sum_all(
        jnp.stack(
            [
                jnp.sum(grad_first_inner * first_normed, axis=(0, 1)),
                jnp.sum(grad_first_inner, axis=(0, 1)),
            ]
        )
    )
    grad_first_gain, grad_first_shift = sums[0], sums[1]
    grad_tokens = grad_summed + norm_back(
        grad_first_inner,
        first_normed,
        first_scale,
        first_gain,
        grad_first_gain,
        grad_first_shift,
        weight,
        counted,
    )
    return (
        block,
        tracks,
        grad_tokens,
        grad_conv,
        grad_point,
        grad_head,
        grad_first_gain,
        grad_first_shift,
        grad_second_gain,
        grad_second_shift,
        grad_point_bias,
        grad_head_bias,
    )


def solution(mesh):
    rows = P("wide", "narrow", None)
    split = P(("wide", "narrow"), None)
    tracks = P("wide", None, "narrow")
    return jax.shard_map(
        shards,
        mesh=mesh,
        in_specs=(
            (rows, P("wide", "narrow"), split, split, split) + (P(),) * 6 + (rows, tracks)
        ),
        out_specs=(rows, tracks, rows, split, split, split) + (P(),) * 6,
        check_vma=False,
    )
```
